1024 devices in a mesh: blk: 256 (over x, y, z_hi), head: 4 (over z_lo, core).
Axes of the slice: x: 8, y: 8, z: 8 (z_hi: 4, z_lo: 2; z = z_hi * 2 + z_lo), core: 2. Of those that a mesh axis runs over, the one named last changes fastest.
Arguments:
- queries: bfloat16 [131072, 2048], P(('blk', 'head')), may hold values from -8 to 8
- key_feats: bfloat16 [131072, 2048], P(('blk', 'head')), may hold values from -8 to 8
- value_feats: bfloat16 [131072, 2048], P(('blk', 'head')), may hold values from -6 to 6
- segment_ids: int32 [131072], P(('blk', 'head')), may hold values from 0 to 511, never falling along the last dimension, each value on 1 to 512 neighbouring positions
Outputs:
- attended: bfloat16 [131072, 2048], P(('blk', 'head'))
The draws below stay inside these ranges and needn't reach their ends.
Inputs may be any that keep to these rules, and one draw needn't show every extreme that they name: `segment_ids`: ids never fall along the stream; every id from 0 to 511 names 1 to 512 consecutive tokens, and some document has exactly 512 tokens.
All inputs are finite; a program needn't handle non-finite values.
Results may differ from the reference program's by a relative error of at most 0.0044.
Values may be sent and summed in bfloat16 or wider, within the bound.
No kernel may reach another device: no remote copies, remote signals or barrier semaphores. Data moves between devices by JAX's collectives and lax.ppermute only.
A program may use at most 64 MiB of HBM per device.

```python
import math
import jax
import jax.numpy as jnp
import numpy as np
from jax import lax

HEADS = 16
HD = 128
REACH = 1
BLOCK = 512
TOKENS = 131072
MOST_DOC = 512
DOCS = 512
N_BLK = 256


def draw_queries(key, part):
    base = jnp.clip(jax.random.normal(jax.random.fold_in(key, 1), (TOKENS, HEADS * HD), jnp.float32), -6.0, 6.0)
    return base.astype(jnp.bfloat16)


def draw_key_feats(key, part):
    base = jnp.clip(jax.random.normal(jax.random.fold_in(key, 2), (TOKENS, HEADS * HD), jnp.float32), -6.0, 6.0)
    return base.astype(jnp.bfloat16)


def steps_of(stream_key, dims, pieces, smallest, top_value):
    loudness, own = 1.0, jax.random.fold_in(stream_key, 6)
    for axis_at, shards_of in pieces:
        steps = jnp.exp(jax.random.uniform(jax.random.fold_in(own, axis_at), (shards_of,), jnp.float32, smallest / len(pieces), top_value / len(pieces)))
        loudness = loudness * jnp.repeat(steps, dims[axis_at] // shards_of).reshape([-1 if axis == axis_at else 1 for axis in range(len(dims))])
    return loudness


def split_up(count, total, bound, lean):
    weights = [(1 << 20) // math.isqrt(grade ** lean) + 1 for grade in range(2, count + 1)]
    rest, given = total - bound - (count - 1), [1] * (count - 1)
    while rest > 0:
        free = [i for i in range(count - 1) if given[i] < bound]
        mass, left = sum([weights[i] for i in free]), rest
        for i in free:
            more = min(bound - given[i], max(1, left * weights[i] // mass), rest)
            given[i] = given[i] + more
            rest = rest - more
    return np.array([bound] + given)


def ragged(own_key, number_of, total, limit, lean):
    if number_of == 2:
        one = jax.random.randint(own_key, (), max(1, total - limit), min(limit, total - 1) + 1)
        return jnp.stack([one, total - one])
    lengths = jnp.asarray(split_up(number_of, total, limit, lean), jnp.int32)
    couples = (number_of - 1) // 2
    giver, receiver = lengths[1:1 + 2 * couples:2], lengths[2:2 + 2 * couples:2]
    margin = jnp.minimum(giver - 1, limit - receiver)
    shifted = jax.random.randint(jax.random.fold_in(own_key, 1), (couples,), 0, 1 << 20) % (margin + 1)
    lengths = lengths.at[1:1 + 2 * couples:2].set(giver - shifted).at[2:2 + 2 * couples:2].set(receiver + shifted)
    return lengths[jax.random.permutation(jax.random.fold_in(own_key, 2), number_of)]


def centred(stream_key, shape, spread, reach, split=(), held_as=jnp.bfloat16):
    loudness = steps_of(stream_key, shape, split, -0.22, 0.18) if split else 1.0
    result = jax.random.normal(stream_key, shape, jnp.float32) * spread * loudness
    return jnp.minimum(jnp.maximum(result, -reach), reach).astype(held_as)


def setup_inputs(seed: int = 0) -> dict:
    key_of = jax.random.split(jax.random.key(seed), 5)
    queries = draw_queries(jax.random.fold_in(key_of[4], 71), 0)
    key_feats = draw_key_feats(jax.random.fold_in(key_of[4], 71), 0)
    value_feats = centred(key_of[2], (TOKENS, HEADS * HD), 1.0, 6.0, ((0, 1024),))
    segment_ids = jnp.searchsorted(jnp.cumsum(ragged(key_of[3], DOCS, TOKENS, MOST_DOC, 2)), jnp.arange(TOKENS), side="right").astype(jnp.int32)
    return dict(queries=queries, key_feats=key_feats, value_feats=value_feats, segment_ids=segment_ids)


def reference(queries, key_feats, value_feats, segment_ids):
    feature_width = HEADS * HD
    margin_rows = REACH * BLOCK
    window_rows = (2 * REACH + 1) * BLOCK
    keys_padded = jnp.pad(key_feats, ((margin_rows, margin_rows), (0, 0)))
    values_padded = jnp.pad(value_feats, ((margin_rows, margin_rows), (0, 0)))
    ids_padded = jnp.pad(segment_ids, (margin_rows, margin_rows), constant_values=-1)

    def one_block(block_index):
        row_start = (block_index * BLOCK).astype(jnp.int32)
        query_rows = lax.dynamic_slice_in_dim(queries, row_start, BLOCK, 0)
        query_ids = lax.dynamic_slice_in_dim(segment_ids, row_start, BLOCK, 0)
        key_rows = lax.dynamic_slice_in_dim(keys_padded, row_start, window_rows, 0)
        value_rows = lax.dynamic_slice_in_dim(values_padded, row_start, window_rows, 0)
        key_ids = lax.dynamic_slice_in_dim(ids_padded, row_start, window_rows, 0)
        allowed = (query_ids[:, None] == key_ids[None, :])[None, :, :]
        query_heads = query_rows.reshape(BLOCK, HEADS, HD).astype(jnp.float32)
        key_heads = key_rows.reshape(window_rows, HEADS, HD).astype(jnp.float32)
        value_heads = value_rows.reshape(window_rows, HEADS, HD).astype(jnp.float32)
        scores = jnp.einsum('qhd,khd->hqk', query_heads, key_heads) / math.sqrt(HD)
        row_max = lax.optimization_barrier(jnp.max(jnp.where(allowed, scores, -jnp.inf), axis=2, keepdims=True))
        exp_scores = jnp.where(allowed, jnp.exp(scores - row_max), 0.0)
        row_total = lax.optimization_barrier(jnp.sum(exp_scores, axis=2, keepdims=True))
        weights = exp_scores.astype(jnp.bfloat16).astype(jnp.float32)
        summed = jnp.einsum('hqk,khd->hqd', weights, value_heads) / row_total
        return jnp.transpose(summed, (1, 0, 2)).reshape(BLOCK, feature_width).astype(jnp.bfloat16)
    blocks = lax.map(one_block, jnp.arange(N_BLK, dtype=jnp.int32))
    return blocks.reshape(TOKENS, feature_width)
```

```python
import functools
import math

import jax
import jax.numpy as jnp
from jax import lax
from jax.experimental import pallas as pl
from jax.experimental.pallas import tpu as pltpu
from jax.sharding import PartitionSpec as P

HD = 128
AXES = ("blk", "head")
NEG = -1e30
F32 = jnp.float32
BF16 = jnp.bfloat16


def pack_kernel(core_ref, k_mine, v_mine, k_other, v_other, q_mine, q_other, ids_ref, kv_out, kvq_out, q_out):
    tokens = k_mine.shape[0]
    heads = k_mine.shape[1] // HD
    full = heads * tokens
    for head in range(heads):
        cols = slice(head * HD, (head + 1) * HD)
        rows = head * tokens
        kv_out[rows : rows + tokens, :] = k_mine[:, cols]
        kv_out[full + rows : full + rows + tokens, :] = v_mine[:, cols]
        kvq_out[rows : rows + tokens, :] = k_other[:, cols]
        kvq_out[full + rows : full + rows + tokens, :] = v_other[:, cols]
        kvq_out[2 * full + 16 + rows : 2 * full + 16 + rows + tokens, :] = q_other[:, cols]
        q_out[rows : rows + tokens, :] = q_mine[:, cols]
    ids = ids_ref[...] + 1
    row = lax.broadcasted_iota(jnp.int32, (16, tokens), 0)
    tile = jnp.where(row == 0, ids >> 4, jnp.where(row == 1, ids & 15, 0)).astype(F32).astype(BF16)
    kv_out[2 * full : 2 * full + 16, :] = tile
    kvq_out[2 * full : 2 * full + 16, :] = tile


def pack(core, queries, keys, values, ids):
    tokens, width = queries.shape
    half = width // 2
    heads = half // HD
    mine = pl.BlockSpec((tokens, half), lambda i, c: (0, c[0]))
    other = pl.BlockSpec((tokens, half), lambda i, c: (0, 1 - c[0]))
    rows = heads * tokens

    def whole(n):
        return pl.BlockSpec((n, HD), lambda i, c: (0, 0))

    return pl.pallas_call(
        pack_kernel,
        grid_spec=pltpu.PrefetchScalarGridSpec(
            num_scalar_prefetch=1,
            grid=(1,),
            in_specs=[mine, mine, other, other, mine, other, pl.BlockSpec((1, tokens), lambda i, c: (0, 0))],
            out_specs=[whole(2 * rows + 16), whole(3 * rows + 16), whole(rows)],
        ),
        out_shape=[
            jax.ShapeDtypeStruct((2 * rows + 16, HD), BF16),
            jax.ShapeDtypeStruct((3 * rows + 16, HD), BF16),
            jax.ShapeDtypeStruct((rows, HD), BF16),
        ],
        name="pack",
    )(core, keys, values, keys, values, queries, queries, ids)


def id_row(ref, at):
    tile = ref[at : at + 16, :].astype(F32)
    return tile[0:1, :] * 16.0 + tile[1:2, :]


def attend_kernel(heads, tokens, groups, n_buf, first, last, core_ref, *refs):
    refs = list(refs)
    qs = [refs.pop(0) for _ in range(groups)]
    qids = [refs.pop(0) for _ in range(groups)]
    bufs = [refs.pop(0) for _ in range(n_buf)]
    carry = [] if first else [(refs.pop(0), refs.pop(0)) for _ in range(groups)]
    if last:
        outs = [refs.pop(0) for _ in range(groups)]
    else:
        outs = [(refs.pop(0), refs.pop(0)) for _ in range(groups)]
    biases = [refs.pop(0) for _ in range(groups)]
    full = heads * tokens
    at = 2 * full
    scale = 1.0 / (math.sqrt(HD) * math.log(2.0))
    key_ids = [id_row(b, at) for b in bufs]
    for g in range(groups):
        column = jnp.broadcast_to(id_row(qids[g], at), (tokens, tokens)).T
        for b in range(n_buf):
            biases[g][:, b * tokens : (b + 1) * tokens] = jnp.where(column == key_ids[b], 0.0, NEG)

    def one_head(head, _):
        rows = pl.ds(pl.multiple_of(head * tokens, tokens), tokens)
        v_rows = pl.ds(pl.multiple_of(full + head * tokens, tokens), tokens)
        keys = jnp.concatenate([b[rows, :] for b in bufs], axis=0)
        vals = jnp.concatenate([b[v_rows, :] for b in bufs], axis=0)
        for g in range(groups):
            q_at = rows if qs[g].shape[0] == full else pl.ds(pl.multiple_of(2 * full + 16 + head * tokens, 16), tokens)
            s = lax.dot_general(qs[g][q_at, :], keys, (((1,), (1,)), ((), ())), preferred_element_type=F32)
            s = s * scale + biases[g][...]
            m = jnp.max(s, axis=1, keepdims=True)
            if not first:
                old_acc, old_stat = carry[g]
                stat = old_stat[rows, :]
                old_m, old_l = stat[:, 0:1], stat[:, 1:2]
                m = jnp.maximum(m, old_m)
                alpha = jnp.exp2(old_m - m)
            p = jnp.exp2(s - m)
            l = jnp.sum(p, axis=1, keepdims=True)
            acc = jnp.dot(p.astype(BF16), vals, preferred_element_type=F32)
            if not first:
                l = l + alpha * old_l
                acc = acc + alpha * old_acc[rows, :]
            if last:
                outs[g][rows, :] = (acc / l).astype(BF16)
            else:
                new_acc, new_stat = outs[g]
                new_acc[rows, :] = acc
                lane = lax.broadcasted_iota(jnp.int32, (tokens, HD), 1)
                new_stat[rows, :] = jnp.where(lane == 0, m, l)
        return 0

    lax.fori_loop(0, heads, one_head, 0)


def attend(qs, qids, bufs, carry, last, name):
    groups, n_buf = len(qs), len(bufs)
    tokens = 128
    heads = (qids[0].shape[0] - 16) // tokens // 2 if qids[0].shape[0] < 3000 else (qids[0].shape[0] - 16) // tokens // 3
    rows = heads * tokens
    first = not carry
    flat_carry = [x for pair in carry for x in pair]
    if last:
        shapes = [jax.ShapeDtypeStruct((rows, HD), BF16) for _ in range(groups)]
    else:
        shapes = [jax.ShapeDtypeStruct((rows, HD), F32) for _ in range(2 * groups)]
    vmem = pl.BlockSpec(memory_space=pltpu.VMEM)
    elements = groups * rows * n_buf * tokens
    out = pl.pallas_call(
        functools.partial(attend_kernel, heads, tokens, groups, n_buf, first, last, None),
        in_specs=[vmem] * (2 * groups + n_buf + len(flat_carry)),
        out_specs=[vmem] * len(shapes),
        out_shape=shapes,
        scratch_shapes=[pltpu.VMEM((tokens, n_buf * tokens), F32) for _ in range(groups)],
        cost_estimate=pl.CostEstimate(flops=elements * 512, bytes_accessed=n_buf * rows * 512 + groups * rows * 1024, transcendentals=elements),
        name=name,
    )(*qs, *qids, *bufs, *flat_carry)
    if last:
        return out
    return [(out[2 * g], out[2 * g + 1]) for g in range(groups)]


def place_kernel(core_ref, o_mine, o_back, out_ref):
    tokens = out_ref.shape[0]
    half = out_ref.shape[1] // 2
    heads = half // HD
    core = core_ref[0]
    for side in range(2):
        @pl.when(core == side)
        def _():
            for head in range(heads):
                rows = slice(head * tokens, (head + 1) * tokens)
                a = side * half + head * HD
                b = (1 - side) * half + head * HD
                out_ref[:, a : a + HD] = o_mine[rows, :]
                out_ref[:, b : b + HD] = o_back[rows, :]


def place(core, o_mine, o_back, tokens, width):
    vmem = pl.BlockSpec(memory_space=pltpu.VMEM)
    return pl.pallas_call(
        place_kernel,
        in_specs=[pl.BlockSpec(memory_space=pltpu.SMEM), vmem, vmem],
        out_specs=vmem,
        out_shape=jax.ShapeDtypeStruct((tokens, width), BF16),
        name="place",
    )(core, o_mine, o_back)


def shards(queries, key_feats, value_feats, segment_ids):
    count = lax.axis_size(AXES)
    tokens, width = queries.shape
    core = lax.axis_index("head") % 2
    core_arr = core.reshape(1).astype(jnp.int32)

    def shift(x, steps):
        return lax.ppermute(x, AXES, [(d, (d + steps) % count) for d in range(count)])

    def swap(x):
        return lax.ppermute(x, AXES, [(d, d ^ 1) for d in range(count)])

    kv, kvq, q = pack(core_arr, queries, key_feats, value_feats, segment_ids.reshape(1, tokens))
    up1 = shift(kv, 2)
    down1 = shift(kv, -2)
    kvq2 = swap(kvq)
    kv2 = kvq2[: kv.shape[0]]
    up1b = shift(kv2, 2)
    down1b = shift(kv2, -2)
    up2 = shift(up1, 2)
    down2 = shift(down1, -2)
    up2b = shift(up1b, 2)
    down2b = shift(down1b, -2)
    qs, qids = [q, kvq2], [kv, kvq2]
    carry = attend([q, kvq2], [kv, kv2], [kv, kv2, up1, down1], [], False, "attend_a")
    carry = attend([q, kvq2], [kv, kv2], [up1b, down1b], carry, False, "attend_b")
    carry = attend([q, kvq2], [kv, kv2], [up2, down2], carry, False, "attend_c")
    (o_other,) = attend([kvq2], [kv2], [up2b, down2b], [carry[1]], True, "attend_d")
    back = swap(o_other)
    (o_mine,) = attend([q], [kv], [up2b, down2b], [carry[0]], True, "attend_e")
    return place(core_arr, o_mine, back, tokens, width)


def solution(mesh):
    return jax.shard_map(
        shards,
        mesh=mesh,
        in_specs=(
            P(("blk", "head"), None),
            P(("blk", "head"), None),
            P(("blk", "head"), None),
            P(("blk", "head")),
        ),
        out_specs=P(("blk", "head"), None),
        check_vma=False,
    )
```

```python
import functools
import math

import jax
import jax.numpy as jnp
from jax import lax
from jax.experimental import pallas as pl
from jax.experimental.pallas import tpu as pltpu
from jax.sharding import PartitionSpec as P

HD = 128
AXES = ("blk", "head")
NEG = -1e30
F32 = jnp.float32
BF16 = jnp.bfloat16


def pack_half(k_ref, v_ref, ids_ref, out_ref):
    tokens = k_ref.shape[0]
    heads = k_ref.shape[1] // HD
    full = heads * tokens
    for head in range(heads):
        cols = slice(head * HD, (head + 1) * HD)
        rows = head * tokens
        out_ref[rows : rows + tokens, :] = k_ref[:, cols]
        out_ref[full + rows : full + rows + tokens, :] = v_ref[:, cols].T
    ids = ids_ref[...] + 1
    row = lax.broadcasted_iota(jnp.int32, (16, tokens), 0)
    tile = jnp.where(row == 0, ids >> 4, jnp.where(row == 1, ids & 15, 0)).astype(F32).astype(BF16)
    out_ref[2 * full : 2 * full + 16, :] = tile


def pack_mine_kernel(core_ref, k_ref, v_ref, ids_ref, kv_out):
    pack_half(k_ref, v_ref, ids_ref, kv_out)


def pack_other_kernel(core_ref, k_ref, v_ref, q_other, q_mine, ids_ref, kvq_out, q_out):
    pack_half(k_ref, v_ref, ids_ref, kvq_out)
    tokens = k_ref.shape[0]
    heads = k_ref.shape[1] // HD
    at = 2 * heads * tokens + 16
    for head in range(heads):
        cols = slice(head * HD, (head + 1) * HD)
        rows = head * tokens
        kvq_out[at + rows : at + rows + tokens, :] = q_other[:, cols]
        q_out[rows : rows + tokens, :] = q_mine[:, cols]


def pack(core, queries, keys, values, ids):
    tokens, width = queries.shape
    half = width // 2
    heads = half // HD
    mine = pl.BlockSpec((tokens, half), lambda i, c: (0, c[0]))
    other = pl.BlockSpec((tokens, half), lambda i, c: (0, 1 - c[0]))
    id_spec = pl.BlockSpec((1, tokens), lambda i, c: (0, 0))
    rows = heads * tokens

    def whole(n):
        return pl.BlockSpec((n, HD), lambda i, c: (0, 0))

    def call(kernel, in_specs, sizes, name, *args):
        return pl.pallas_call(
            kernel,
            grid_spec=pltpu.PrefetchScalarGridSpec(
                num_scalar_prefetch=1, grid=(1,), in_specs=in_specs, out_specs=[whole(n) for n in sizes]
            ),
            out_shape=[jax.ShapeDtypeStruct((n, HD), BF16) for n in sizes],
            name=name,
        )(core, *args)

    (kv,) = call(pack_mine_kernel, [mine, mine, id_spec], [2 * rows + 16], "pack_mine", keys, values, ids)
    kvq, q = call(
        pack_other_kernel,
        [other, other, other, mine, id_spec],
        [3 * rows + 16, rows],
        "pack_other",
        keys,
        values,
        queries,
        queries,
        ids,
    )
    return kv, kvq, q


def id_row(ref, at):
    tile = ref[at : at + 16, :].astype(F32)
    return tile[0:1, :] * 16.0 + tile[1:2, :]


def attend_kernel(heads, tokens, groups, n_buf, first, last, *refs):
    refs = list(refs)
    qs = [refs.pop(0) for _ in range(groups)]
    qids = [refs.pop(0) for _ in range(groups)]
    bufs = [refs.pop(0) for _ in range(n_buf)]
    carry = [] if first else [(refs.pop(0), refs.pop(0)) for _ in range(groups)]
    if last:
        outs = [refs.pop(0) for _ in range(groups)]
    else:
        outs = [(refs.pop(0), refs.pop(0)) for _ in range(groups)]
    bias = refs.pop(0)
    full = heads * tokens
    at = 2 * full
    scale = 1.0 / (math.sqrt(HD) * math.log(2.0))
    query_ids = jnp.concatenate([id_row(q, at) for q in qids], axis=1)
    for b in range(n_buf):
        column = jnp.broadcast_to(id_row(bufs[b], at), (tokens, tokens)).T
        column = jnp.concatenate([column] * groups, axis=1)
        bias[b * tokens : (b + 1) * tokens, :] = jnp.where(column == query_ids, 0.0, NEG)
    q_base = [0 if q.shape[0] == full else 2 * full + 16 for q in qs]
    for head in range(heads):
        rows = slice(head * tokens, (head + 1) * tokens)
        v_rows = slice(full + head * tokens, full + (head + 1) * tokens)
        keys = jnp.concatenate([b[rows, :] for b in bufs], axis=0)
        vals = jnp.concatenate([b[v_rows, :] for b in bufs], axis=1)
        query = jnp.concatenate(
            [q[base + head * tokens : base + (head + 1) * tokens, :] for q, base in zip(qs, q_base)], axis=0
        )
        s = lax.dot_general(keys, query, (((1,), (1,)), ((), ())), preferred_element_type=F32)
        s = s * scale + bias[...]
        m = jnp.max(s, axis=0, keepdims=True)
        if not first:
            old_m = jnp.concatenate([stat[head : head + 1, :] for _, stat in carry], axis=1)
            old_l = jnp.concatenate([stat[heads + head : heads + head + 1, :] for _, stat in carry], axis=1)
            old_acc = jnp.concatenate([acc[rows, :] for acc, _ in carry], axis=1)
            m = jnp.maximum(m, old_m)
            alpha = jnp.exp2(old_m - m)
        p = jnp.exp2(s - m)
        l = jnp.sum(p, axis=0, keepdims=True)
        acc = jnp.dot(vals, p.astype(BF16), preferred_element_type=F32)
        if not first:
            l = l + alpha * old_l
            acc = acc + alpha * old_acc
        if last:
            acc = acc * (1.0 / l)
        for g in range(groups):
            lanes = slice(g * tokens, (g + 1) * tokens)
            if last:
                outs[g][rows, :] = acc[:, lanes].T.astype(BF16)
            else:
                new_acc, new_stat = outs[g]
                new_acc[rows, :] = acc[:, lanes]
                new_stat[head : head + 1, :] = m[:, lanes]
                new_stat[heads + head : heads + head + 1, :] = l[:, lanes]


def attend(heads, qs, qids, bufs, carry, last, name):
    groups, n_buf, tokens = len(qs), len(bufs), HD
    rows = heads * tokens
    first = not carry
    flat_carry = [x for pair in carry for x in pair]
    if last:
        shapes = [jax.ShapeDtypeStruct((rows, HD), BF16) for _ in range(groups)]
    else:
        shapes = [jax.ShapeDtypeStruct((n, tokens), F32) for _ in range(groups) for n in (rows, 2 * heads)]
    vmem = pl.BlockSpec(memory_space=pltpu.VMEM)
    elements = groups * rows * n_buf * tokens
    out = pl.pallas_call(
        functools.partial(attend_kernel, heads, tokens, groups, n_buf, first, last),
        in_specs=[vmem] * (2 * groups + n_buf + len(flat_carry)),
        out_specs=[vmem] * len(shapes),
        out_shape=shapes,
        scratch_shapes=[pltpu.VMEM((n_buf * tokens, groups * tokens), F32)],
        cost_estimate=pl.CostEstimate(
            flops=elements * 512, bytes_accessed=n_buf * rows * 512 + groups * rows * 1024, transcendentals=elements
        ),
        name=name,
    )(*qs, *qids, *bufs, *flat_carry)
    if last:
        return out
    return [(out[2 * g], out[2 * g + 1]) for g in range(groups)]


def place_kernel(core_ref, o_mine, o_back, out_ref):
    tokens = out_ref.shape[0]
    half = out_ref.shape[1] // 2
    heads = half // HD
    core = core_ref[0]
    for side in range(2):
        @pl.when(core == side)
        def _():
            for head in range(heads):
                rows = slice(head * tokens, (head + 1) * tokens)
                a = side * half + head * HD
                b = (1 - side) * half + head * HD
                out_ref[:, a : a + HD] = o_mine[rows, :]
                out_ref[:, b : b + HD] = o_back[rows, :]


def place(core, o_mine, o_back, tokens, width):
    vmem = pl.BlockSpec(memory_space=pltpu.VMEM)
    return pl.pallas_call(
        place_kernel,
        in_specs=[pl.BlockSpec(memory_space=pltpu.SMEM), vmem, vmem],
        out_specs=vmem,
        out_shape=jax.ShapeDtypeStruct((tokens, width), BF16),
        name="place",
    )(core, o_mine, o_back)


def shards(queries, key_feats, value_feats, segment_ids):
    count = lax.axis_size(AXES)
    tokens, width = queries.shape
    core = lax.axis_index("head") % 2
    core_arr = core.reshape(1).astype(jnp.int32)

    def shift(x, steps):
        return lax.ppermute(x, AXES, [(d, (d + steps) % count) for d in range(count)])

    def swap(x):
        return lax.ppermute(x, AXES, [(d, d ^ 1) for d in range(count)])

    kv, kvq, q = pack(core_arr, queries, key_feats, value_feats, segment_ids.reshape(1, tokens))
    up1 = shift(kv, 2)
    down1 = shift(kv, -2)
    kvq2 = swap(kvq)
    kv2 = kvq2[: kv.shape[0]]
    up1b = shift(kv2, 2)
    down1b = shift(kv2, -2)
    up2 = shift(up1, 2)
    down2 = shift(down1, -2)
    up2b = shift(up1b, 2)
    down2b = shift(down1b, -2)
    heads = width // 2 // HD
    carry = attend(heads, [q, kvq2], [kv, kv2], [kv, kv2, up1, down1, up1b, down1b], [], False, "attend_near")
    carry = attend(heads, [q, kvq2], [kv, kv2], [up2, down2], carry, False, "attend_far")
    (o_other,) = attend(heads, [kvq2], [kv2], [up2b, down2b], [carry[1]], True, "attend_other")
    back = swap(o_other)
    (o_mine,) = attend(heads, [q], [kv], [up2b, down2b], [carry[0]], True, "attend_mine")
    return place(core_arr, o_mine, back, tokens, width)


def solution(mesh):
    return jax.shard_map(
        shards,
        mesh=mesh,
        in_specs=(
            P(("blk", "head"), None),
            P(("blk", "head"), None),
            P(("blk", "head"), None),
            P(("blk", "head")),
        ),
        out_specs=P(("blk", "head"), None),
        check_vma=False,
    )
```

```python
import functools
import math

import jax
import jax.numpy as jnp
from jax import lax
from jax.experimental import pallas as pl
from jax.experimental.pallas import tpu as pltpu
from jax.sharding import PartitionSpec as P


HD = 128
AXES = ("blk", "head")
NEG = -1e30
VMEM_LIMIT = 16 << 20
F32 = jnp.float32
BF16 = jnp.bfloat16


def pack_half(k_ref, v_ref, ids_ref, out_ref):
    tokens = k_ref.shape[0]
    heads = k_ref.shape[1] // HD
    full = heads * tokens
    for head in range(heads):
        cols = slice(head * HD, (head + 1) * HD)
        rows = head * tokens
        out_ref[rows : rows + tokens, :] = k_ref[:, cols]
        out_ref[full + rows : full + rows + tokens, :] = v_ref[:, cols].T
    ids = ids_ref[...] + 1
    row = lax.broadcasted_iota(jnp.int32, (16, tokens), 0)
    tile = jnp.where(row == 0, ids >> 4, jnp.where(row == 1, ids & 15, 0)).astype(F32).astype(BF16)
    out_ref[2 * full : 2 * full + 16, :] = tile


def pack_mine_kernel(core_ref, k_ref, v_ref, ids_ref, kv_out):
    pack_half(k_ref, v_ref, ids_ref, kv_out)


def pack_other_kernel(core_ref, k_ref, v_ref, q_other, q_mine, ids_ref, kvq_out, q_out):
    pack_half(k_ref, v_ref, ids_ref, kvq_out)
    tokens = k_ref.shape[0]
    heads = k_ref.shape[1] // HD
    at = 2 * heads * tokens + 16
    for head in range(heads):
        cols = slice(head * HD, (head + 1) * HD)
        rows = head * tokens
        kvq_out[at + rows : at + rows + tokens, :] = q_other[:, cols]
        q_out[rows : rows + tokens, :] = q_mine[:, cols]


def pack(core, queries, keys, values, ids):
    tokens, width = queries.shape
    half = width // 2
    heads = half // HD
    mine = pl.BlockSpec((tokens, half), lambda i, c: (0, c[0]))
    other = pl.BlockSpec((tokens, half), lambda i, c: (0, 1 - c[0]))
    id_spec = pl.BlockSpec((1, tokens), lambda i, c: (0, 0))
    rows = heads * tokens

    def whole(n):
        return pl.BlockSpec((n, HD), lambda i, c: (0, 0))

    def call(kernel, in_specs, sizes, *args):
        return pl.pallas_call(
            kernel,
            grid_spec=pltpu.PrefetchScalarGridSpec(
                num_scalar_prefetch=1, grid=(1,), in_specs=in_specs, out_specs=[whole(n) for n in sizes]
            ),
            out_shape=[jax.ShapeDtypeStruct((n, HD), BF16) for n in sizes],
            compiler_params=pltpu.CompilerParams(vmem_limit_bytes=VMEM_LIMIT),
        )(core, *args)

    (kv,) = call(pack_mine_kernel, [mine, mine, id_spec], [2 * rows + 16], keys, values, ids)
    keys, values, queries, kv = lax.optimization_barrier((keys, values, queries, kv))
    kvq, q = call(
        pack_other_kernel,
        [other, other, other, mine, id_spec],
        [3 * rows + 16, rows],
        keys,
        values,
        queries,
        queries,
        ids,
    )
    return kv, kvq, q


def id_row(ref, at):
    tile = ref[at : at + 16, :].astype(F32)
    return tile[0:1, :] * 16.0 + tile[1:2, :]


def attend_kernel(heads, tokens, groups, n_buf, first, last, *refs):
    refs = list(refs)
    qs = [refs.pop(0) for _ in range(groups)]
    qids = [refs.pop(0) for _ in range(groups)]
    bufs = [refs.pop(0) for _ in range(n_buf)]
    carry = [] if first else [(refs.pop(0), refs.pop(0)) for _ in range(groups)]
    if last:
        outs = [refs.pop(0) for _ in range(groups)]
    else:
        outs = [(refs.pop(0), refs.pop(0)) for _ in range(groups)]
    bias = refs.pop(0)
    full = heads * tokens
    at = 2 * full
    scale = 1.0 / (math.sqrt(HD) * math.log(2.0))
    query_ids = jnp.concatenate([id_row(q, at) for q in qids], axis=1)
    for b in range(n_buf):
        column = jnp.broadcast_to(id_row(bufs[b], at), (tokens, tokens)).T
        column = jnp.concatenate([column] * groups, axis=1)
        bias[b * tokens : (b + 1) * tokens, :] = jnp.where(column == query_ids, 0.0, NEG)
    q_base = [0 if q.shape[0] == full else 2 * full + 16 for q in qs]
    for head in range(heads):
        rows = slice(head * tokens, (head + 1) * tokens)
        v_rows = slice(full + head * tokens, full + (head + 1) * tokens)
        keys = jnp.concatenate([b[rows, :] for b in bufs], axis=0)
        vals = jnp.concatenate([b[v_rows, :] for b in bufs], axis=1)
        query = jnp.concatenate(
            [q[base + head * tokens : base + (head + 1) * tokens, :] for q, base in zip(qs, q_base)], axis=0
        )
        s = lax.dot_general(keys, query, (((1,), (1,)), ((), ())), preferred_element_type=F32)
        s = s * scale + bias[...]
        m = jnp.max(s, axis=0, keepdims=True)
        if not first:
            old_m = jnp.concatenate([stat[head : head + 1, :] for _, stat in carry], axis=1)
            old_l = jnp.concatenate([stat[heads + head : heads + head + 1, :] for _, stat in carry], axis=1)
            old_acc = jnp.concatenate([acc[rows, :] for acc, _ in carry], axis=1)
            m = jnp.maximum(m, old_m)
            alpha = jnp.exp2(old_m - m)
        p = jnp.exp2(s - m)
        l = jnp.sum(p, axis=0, keepdims=True)
        acc = jnp.dot(vals, p.astype(BF16), preferred_element_type=F32)
        if not first:
            l = l + alpha * old_l
            acc = acc + alpha * old_acc
        if last:
            acc = acc * (1.0 / l)
        for g in range(groups):
            lanes = slice(g * tokens, (g + 1) * tokens)
            if last:
                outs[g][rows, :] = acc[:, lanes].T.astype(BF16)
            else:
                new_acc, new_stat = outs[g]
                new_acc[rows, :] = acc[:, lanes]
                new_stat[head : head + 1, :] = m[:, lanes]
                new_stat[heads + head : heads + head + 1, :] = l[:, lanes]


def attend(heads, qs, qids, bufs, carry, last):
    groups, n_buf, tokens = len(qs), len(bufs), HD
    rows = heads * tokens
    first = not carry
    flat_carry = [x for pair in carry for x in pair]
    if last:
        shapes = [jax.ShapeDtypeStruct((rows, HD), BF16) for _ in range(groups)]
    else:
        shapes = [jax.ShapeDtypeStruct((n, tokens), F32) for _ in range(groups) for n in (rows, 2 * heads)]
    vmem = pl.BlockSpec(memory_space=pltpu.VMEM)
    elements = groups * rows * n_buf * tokens
    out = pl.pallas_call(
        functools.partial(attend_kernel, heads, tokens, groups, n_buf, first, last),
        in_specs=[vmem] * (2 * groups + n_buf + len(flat_carry)),
        out_specs=[vmem] * len(shapes),
        out_shape=shapes,
        scratch_shapes=[pltpu.VMEM((n_buf * tokens, groups * tokens), F32)],
        cost_estimate=pl.CostEstimate(
            flops=elements * 512, bytes_accessed=n_buf * rows * 512 + groups * rows * 1024, transcendentals=elements
        ),
        compiler_params=pltpu.CompilerParams(vmem_limit_bytes=VMEM_LIMIT),
    )(*qs, *qids, *bufs, *flat_carry)
    if last:
        return out
    return [(out[2 * g], out[2 * g + 1]) for g in range(groups)]


def place_kernel(core_ref, o_mine, o_back, out_ref):
    tokens = out_ref.shape[0]
    half = out_ref.shape[1] // 2
    heads = half // HD
    core = core_ref[0]
    for side in range(2):
        @pl.when(core == side)
        def _():
            for head in range(heads):
                rows = slice(head * tokens, (head + 1) * tokens)
                a = side * half + head * HD
                b = (1 - side) * half + head * HD
                out_ref[:, a : a + HD] = o_mine[rows, :]
                out_ref[:, b : b + HD] = o_back[rows, :]


def place(core, o_mine, o_back, tokens, width):
    vmem = pl.BlockSpec(memory_space=pltpu.VMEM)
    return pl.pallas_call(
        place_kernel,
        in_specs=[pl.BlockSpec(memory_space=pltpu.SMEM), vmem, vmem],
        out_specs=vmem,
        out_shape=jax.ShapeDtypeStruct((tokens, width), BF16),
        compiler_params=pltpu.CompilerParams(vmem_limit_bytes=VMEM_LIMIT),
        name="place",
    )(core, o_mine, o_back)


def layer(queries, key_feats, value_feats, segment_ids):
    count = lax.axis_size(AXES)
    tokens, width = queries.shape
    core = lax.axis_index("head") % 2
    core_arr = core.reshape(1).astype(jnp.int32)

    def shift(x, steps):
        return lax.ppermute(x, AXES, [(d, (d + steps) % count) for d in range(count)])

    def swap(x):
        return lax.ppermute(x, AXES, [(d, d ^ 1) for d in range(count)])

    kv, kvq, q = pack(core_arr, queries, key_feats, value_feats, segment_ids.reshape(1, tokens))
    up1 = shift(kv, 2)
    down1 = shift(kv, -2)
    kvq2 = swap(kvq)
    kv2 = kvq2[: kv.shape[0]]
    up1b = shift(kv2, 2)
    down1b = shift(kv2, -2)
    heads = width // 2 // HD
    qs, qids = [q, kvq2], [kv, kv2]
    carry = attend(heads, qs, qids, [kv, kv2], [], False)
    up1, down1, carry = lax.optimization_barrier((up1, down1, carry))
    up2 = shift(up1, 2)
    down2 = shift(down1, -2)
    carry = attend(heads, qs, qids, [up1, down1], carry, False)
    up1b, down1b, carry = lax.optimization_barrier((up1b, down1b, carry))
    up2b = shift(up1b, 2)
    down2b = shift(down1b, -2)
    carry = attend(heads, qs, qids, [up1b, down1b, up2, down2], carry, False)
    (o_other,) = attend(heads, [kvq2], [kv2], [up2b, down2b], [carry[1]], True)
    back = swap(o_other)
    (o_mine,) = attend(heads, [q], [kv], [up2b, down2b], [carry[0]], True)
    return place(core_arr, o_mine, back, tokens, width)


def solution(mesh):
    return jax.shard_map(
        layer,
        mesh=mesh,
        in_specs=(
            P(("blk", "head"), None),
            P(("blk", "head"), None),
            P(("blk", "head"), None),
            P(("blk", "head")),
        ),
        out_specs=P(("blk", "head"), None),
        check_vma=False,
    )
```

```python
import functools
import math

import jax
import jax.numpy as jnp
from jax import lax
from jax.experimental import pallas as pl
from jax.experimental.pallas import tpu as pltpu
from jax.sharding import PartitionSpec as P


HD = 128
AXES = ("blk", "head")
NEG = -1e30
VMEM_LIMIT = 16 << 20
WHOLE_VMEM = 67043328
F32 = jnp.float32
BF16 = jnp.bfloat16


def load_halves(loads, sems):
    copies = []
    for n, (source, half_index, dest, at) in enumerate(loads):
        tokens, width = source.shape
        heads = width // 2 // HD
        for head in range(heads):
            first_col = pl.multiple_of(half_index * (width // 2) + head * HD, HD)
            rows = slice(at + head * tokens, at + (head + 1) * tokens)
            copy = pltpu.make_async_copy(source.at[:, pl.ds(first_col, HD)], dest.at[rows, :], sems.at[n, head])
            copy.start()
            copies.append(copy)
    return copies


def finish_pack(ids_ref, v_buf, out_ref, v_copies):
    tokens = ids_ref.shape[1]
    heads = v_buf.shape[0] // tokens
    full = heads * tokens
    ids = ids_ref[...] + 1
    row = lax.broadcasted_iota(jnp.int32, (16, tokens), 0)
    tile = jnp.where(row == 0, ids >> 4, jnp.where(row == 1, ids & 15, 0)).astype(F32).astype(BF16)
    out_ref[2 * full : 2 * full + 16, :] = tile
    for head in range(heads):
        v_copies[head].wait()
        rows = head * tokens
        out_ref[full + rows : full + rows + tokens, :] = v_buf[rows : rows + tokens, :].T


def pack_mine_kernel(core_ref, k_hbm, v_hbm, ids_hbm, out_ref, v_buf, ids_buf, sems, id_sem):
    core = core_ref[0]
    heads = k_hbm.shape[1] // 2 // HD
    id_copy = pltpu.make_async_copy(ids_hbm, ids_buf, id_sem)
    id_copy.start()
    copies = load_halves([(v_hbm, core, v_buf, 0), (k_hbm, core, out_ref, 0)], sems)
    id_copy.wait()
    finish_pack(ids_buf, v_buf, out_ref, copies[:heads])
    for copy in copies[heads:]:
        copy.wait()


def pack_other_kernel(core_ref, k_hbm, v_hbm, q_hbm, ids_hbm, out_ref, q_out, v_buf, ids_buf, sems, id_sem):
    core = core_ref[0]
    tokens = k_hbm.shape[0]
    heads = k_hbm.shape[1] // 2 // HD
    at = 2 * heads * tokens + 16
    id_copy = pltpu.make_async_copy(ids_hbm, ids_buf, id_sem)
    id_copy.start()
    copies = load_halves(
        [(v_hbm, 1 - core, v_buf, 0), (k_hbm, 1 - core, out_ref, 0), (q_hbm, 1 - core, out_ref, at), (q_hbm, core, q_out, 0)], sems
    )
    id_copy.wait()
    finish_pack(ids_buf, v_buf, out_ref, copies[:heads])
    for copy in copies[heads:]:
        copy.wait()


def pack(core, queries, keys, values, ids):
    tokens, width = queries.shape
    heads = width // 2 // HD
    rows = heads * tokens
    hbm = pl.BlockSpec(memory_space=pltpu.HBM)
    vmem = pl.BlockSpec(memory_space=pltpu.VMEM)

    def call(kernel, n_loads, sizes, limit, *args):
        return pl.pallas_call(
            kernel,
            in_specs=[pl.BlockSpec(memory_space=pltpu.SMEM)] + [hbm] * len(args),
            out_specs=[vmem for n in sizes],
            out_shape=[jax.ShapeDtypeStruct((n, HD), BF16) for n in sizes],
            scratch_shapes=[
                pltpu.VMEM((rows, HD), BF16),
                pltpu.VMEM((1, tokens), jnp.int32),
                pltpu.SemaphoreType.DMA((n_loads, heads)),
                pltpu.SemaphoreType.DMA(()),
            ],
            compiler_params=pltpu.CompilerParams(vmem_limit_bytes=limit),
        )(core, *args)

    (kv,) = call(pack_mine_kernel, 2, [2 * rows + 16], WHOLE_VMEM, keys, values, ids)
    keys, values, queries, kv = lax.optimization_barrier((keys, values, queries, kv))
    kvq, q = call(pack_other_kernel, 4, [3 * rows + 16, rows], WHOLE_VMEM, keys, values, queries, ids)
    return kv, kvq, q


def id_row(ref, at):
    tile = ref[at : at + 16, :].astype(F32)
    return tile[0:1, :] * 16.0 + tile[1:2, :]


def attend_kernel(heads, tokens, groups, n_buf, first, last, *refs):
    refs = list(refs)
    qs = [refs.pop(0) for _ in range(groups)]
    qids = [refs.pop(0) for _ in range(groups)]
    bufs = [refs.pop(0) for _ in range(n_buf)]
    carry = [] if first else [(refs.pop(0), refs.pop(0)) for _ in range(groups)]
    if last:
        outs = [refs.pop(0) for _ in range(groups)]
    else:
        outs = [(refs.pop(0), refs.pop(0)) for _ in range(groups)]
    bias = refs.pop(0)
    full = heads * tokens
    at = 2 * full
    scale = 1.0 / (math.sqrt(HD) * math.log(2.0))
    query_ids = jnp.concatenate([id_row(q, at) for q in qids], axis=1)
    for b in range(n_buf):
        column = jnp.broadcast_to(id_row(bufs[b], at), (tokens, tokens)).T
        column = jnp.concatenate([column] * groups, axis=1)
        bias[b * tokens : (b + 1) * tokens, :] = jnp.where(column == query_ids, 0.0, NEG)
    q_base = [0 if q.shape[0] == full else 2 * full + 16 for q in qs]
    for head in range(heads):
        rows = slice(head * tokens, (head + 1) * tokens)
        v_rows = slice(full + head * tokens, full + (head + 1) * tokens)
        keys = jnp.concatenate([b[rows, :] for b in bufs], axis=0)
        vals = jnp.concatenate([b[v_rows, :] for b in bufs], axis=1)
        query = jnp.concatenate(
            [q[base + head * tokens : base + (head + 1) * tokens, :] for q, base in zip(qs, q_base)], axis=0
        )
        s = lax.dot_general(keys, query, (((1,), (1,)), ((), ())), preferred_element_type=F32)
        s = s * scale + bias[...]
        m = jnp.max(s, axis=0, keepdims=True)
        if not first:
            old_m = jnp.concatenate([stat[head : head + 1, :] for _, stat in carry], axis=1)
            old_l = jnp.concatenate([stat[heads + head : heads + head + 1, :] for _, stat in carry], axis=1)
            old_acc = jnp.concatenate([acc[rows, :] for acc, _ in carry], axis=1)
            m = jnp.maximum(m, old_m)
            alpha = jnp.exp2(old_m - m)
        p = jnp.exp2(s - m)
        l = jnp.sum(p, axis=0, keepdims=True)
        acc = jnp.dot(vals, p.astype(BF16), preferred_element_type=F32)
        if not first:
            l = l + alpha * old_l
            acc = acc + alpha * old_acc
        if last:
            acc = acc * (1.0 / l)
        for g in range(groups):
            lanes = slice(g * tokens, (g + 1) * tokens)
            if last:
                outs[g][rows, :] = acc[:, lanes].T.astype(BF16)
            else:
                new_acc, new_stat = outs[g]
                new_acc[rows, :] = acc[:, lanes]
                new_stat[head : head + 1, :] = m[:, lanes]
                new_stat[heads + head : heads + head + 1, :] = l[:, lanes]


def attend(heads, qs, qids, bufs, carry, last):
    groups, n_buf, tokens = len(qs), len(bufs), HD
    rows = heads * tokens
    first = not carry
    flat_carry = [x for pair in carry for x in pair]
    if last:
        shapes = [jax.ShapeDtypeStruct((rows, HD), BF16) for _ in range(groups)]
    else:
        shapes = [jax.ShapeDtypeStruct((n, tokens), F32) for _ in range(groups) for n in (rows, 2 * heads)]
    vmem = pl.BlockSpec(memory_space=pltpu.VMEM)
    elements = groups * rows * n_buf * tokens
    out = pl.pallas_call(
        functools.partial(attend_kernel, heads, tokens, groups, n_buf, first, last),
        in_specs=[vmem] * (2 * groups + n_buf + len(flat_carry)),
        out_specs=[vmem] * len(shapes),
        out_shape=shapes,
        scratch_shapes=[pltpu.VMEM((n_buf * tokens, groups * tokens), F32)],
        cost_estimate=pl.CostEstimate(
            flops=elements * 512, bytes_accessed=n_buf * rows * 512 + groups * rows * 1024, transcendentals=elements
        ),
        compiler_params=pltpu.CompilerParams(vmem_limit_bytes=VMEM_LIMIT),
    )(*qs, *qids, *bufs, *flat_carry)
    if last:
        return out
    return [(out[2 * g], out[2 * g + 1]) for g in range(groups)]


def place_kernel(core_ref, o_mine, o_back, out_ref):
    tokens = out_ref.shape[0]
    half = out_ref.shape[1] // 2
    heads = half // HD
    core = core_ref[0]
    for side in range(2):
        @pl.when(core == side)
        def _():
            for head in range(heads):
                rows = slice(head * tokens, (head + 1) * tokens)
                a = side * half + head * HD
                b = (1 - side) * half + head * HD
                out_ref[:, a : a + HD] = o_mine[rows, :]
                out_ref[:, b : b + HD] = o_back[rows, :]


def place(core, o_mine, o_back, tokens, width):
    vmem = pl.BlockSpec(memory_space=pltpu.VMEM)
    return pl.pallas_call(
        place_kernel,
        in_specs=[pl.BlockSpec(memory_space=pltpu.SMEM), vmem, vmem],
        out_specs=vmem,
        out_shape=jax.ShapeDtypeStruct((tokens, width), BF16),
        compiler_params=pltpu.CompilerParams(vmem_limit_bytes=VMEM_LIMIT),
        name="place",
    )(core, o_mine, o_back)


def layer(queries, key_feats, value_feats, segment_ids):
    count = lax.axis_size(AXES)
    tokens, width = queries.shape
    core = lax.axis_index("head") % 2
    core_arr = core.reshape(1).astype(jnp.int32)

    chips = count // 2

    def swap(x):
        return lax.ppermute(x, AXES, [(d, d ^ 1) for d in range(count)])

    def pair_a(x):
        return lax.ppermute(x, AXES, [(d, d ^ 2) for d in range(count)])

    def pair_b(x):
        ups = [(2 * c + i, 2 * c + 2 + i) for c in range(1, chips - 1, 2) for i in range(2)]
        return lax.ppermute(x, AXES, ups + [(v, u) for u, v in ups])

    kv, kvq, q = pack(core_arr, queries, key_feats, value_feats, segment_ids.reshape(1, tokens))
    a1 = pair_a(kv)
    b1 = pair_b(kv)
    kvq2 = swap(kvq)
    kv2 = kvq2[: kv.shape[0]]
    a1b = pair_a(kv2)
    b1b = pair_b(kv2)
    heads = width // 2 // HD
    qs, qids = [q, kvq2], [kv, kv2]
    carry = attend(heads, qs, qids, [kv, kv2], [], False)
    a1, b1, carry = lax.optimization_barrier((a1, b1, carry))
    a2 = pair_a(b1)
    b2 = pair_b(a1)
    carry = attend(heads, qs, qids, [a1, b1], carry, False)
    a1b, b1b, carry = lax.optimization_barrier((a1b, b1b, carry))
    a2b = pair_a(b1b)
    b2b = pair_b(a1b)
    carry = attend(heads, qs, qids, [a1b, b1b, a2, b2], carry, False)
    (o_other,) = attend(heads, [kvq2], [kv2], [a2b, b2b], [carry[1]], True)
    back = swap(o_other)
    (o_mine,) = attend(heads, [q], [kv], [a2b, b2b], [carry[0]], True)
    return place(core_arr, o_mine, back, tokens, width)


def solution(mesh):
    return jax.shard_map(
        layer,
        mesh=mesh,
        in_specs=(
            P(("blk", "head"), None),
            P(("blk", "head"), None),
            P(("blk", "head"), None),
            P(("blk", "head")),
        ),
        out_specs=P(("blk", "head"), None),
        check_vma=False,
    )
```

```python
import functools
import math

import jax
import jax.numpy as jnp
from jax import lax
from jax.experimental import pallas as pl
from jax.experimental.pallas import tpu as pltpu
from jax.sharding import PartitionSpec as P


HD = 128
AXES = ("blk", "head")
NEG = -1e30
VMEM_LIMIT = 16 << 20
WHOLE_VMEM = 67043328
F32 = jnp.float32
BF16 = jnp.bfloat16


def load_halves(loads, sems):
    copies = []
    for n, (source, half_index, dest, at) in enumerate(loads):
        tokens, width = source.shape
        heads = width // 2 // HD
        for head in range(heads):
            first_col = pl.multiple_of(half_index * (width // 2) + head * HD, HD)
            rows = slice(at + head * tokens, at + (head + 1) * tokens)
            copy = pltpu.make_async_copy(source.at[:, pl.ds(first_col, HD)], dest.at[rows, :], sems.at[n, head])
            copy.start()
            copies.append(copy)
    return copies


def finish_pack(ids_ref, v_buf, out_refs, v_copies):
    tokens = ids_ref.shape[1]
    heads = v_buf.shape[0] // tokens
    full = heads * tokens
    ids = ids_ref[...] + 1
    row = lax.broadcasted_iota(jnp.int32, (16, tokens), 0)
    tile = jnp.where(row == 0, ids >> 4, jnp.where(row == 1, ids & 15, 0)).astype(F32).astype(BF16)
    for out_ref in out_refs:
        out_ref[2 * full : 2 * full + 16, :] = tile
    for head in range(heads):
        v_copies[head].wait()
        rows = head * tokens
        turned = v_buf[rows : rows + tokens, :].T
        for out_ref in out_refs:
            out_ref[full + rows : full + rows + tokens, :] = turned


def pack_mine_kernel(core_ref, k_hbm, v_hbm, ids_hbm, out_ref, v_buf, ids_buf, sems, id_sem):
    core = core_ref[0]
    heads = k_hbm.shape[1] // 2 // HD
    id_copy = pltpu.make_async_copy(ids_hbm, ids_buf, id_sem)
    id_copy.start()
    copies = load_halves([(v_hbm, core, v_buf, 0), (k_hbm, core, out_ref, 0)], sems)
    id_copy.wait()
    finish_pack(ids_buf, v_buf, [out_ref], copies[:heads])
    for copy in copies[heads:]:
        copy.wait()


def pack_other_kernel(core_ref, k_hbm, v_hbm, q_hbm, ids_hbm, kv_ref, kvq_ref, q_out, v_buf, ids_buf, sems, id_sem):
    core = core_ref[0]
    tokens = k_hbm.shape[0]
    heads = k_hbm.shape[1] // 2 // HD
    at = 2 * heads * tokens + 16
    id_copy = pltpu.make_async_copy(ids_hbm, ids_buf, id_sem)
    id_copy.start()
    loads = [
        (v_hbm, 1 - core, v_buf, 0),
        (k_hbm, 1 - core, kv_ref, 0),
        (k_hbm, 1 - core, kvq_ref, 0),
        (q_hbm, 1 - core, kvq_ref, at),
        (q_hbm, core, q_out, 0),
    ]
    copies = load_halves(loads, sems)
    id_copy.wait()
    finish_pack(ids_buf, v_buf, [kv_ref, kvq_ref], copies[:heads])
    for copy in copies[heads:]:
        copy.wait()


def pack(core, queries, keys, values, ids):
    tokens, width = queries.shape
    heads = width // 2 // HD
    rows = heads * tokens
    hbm = pl.BlockSpec(memory_space=pltpu.HBM)
    vmem = pl.BlockSpec(memory_space=pltpu.VMEM)

    def call(kernel, n_loads, sizes, limit, *args):
        return pl.pallas_call(
            kernel,
            in_specs=[pl.BlockSpec(memory_space=pltpu.SMEM)] + [hbm] * len(args),
            out_specs=[vmem for n in sizes],
            out_shape=[jax.ShapeDtypeStruct((n, HD), BF16) for n in sizes],
            scratch_shapes=[
                pltpu.VMEM((rows, HD), BF16),
                pltpu.VMEM((1, tokens), jnp.int32),
                pltpu.SemaphoreType.DMA((n_loads, heads)),
                pltpu.SemaphoreType.DMA(()),
            ],
            compiler_params=pltpu.CompilerParams(vmem_limit_bytes=limit),
        )(core, *args)

    (kv,) = call(pack_mine_kernel, 2, [2 * rows + 16], WHOLE_VMEM, keys, values, ids)
    keys, values, queries, kv = lax.optimization_barrier((keys, values, queries, kv))
    kvo, kvq, q = call(pack_other_kernel, 5, [2 * rows + 16, 3 * rows + 16, rows], WHOLE_VMEM, keys, values, queries, ids)
    return kv, kvo, kvq, q


def id_row(ref, at):
    tile = ref[at : at + 16, :].astype(F32)
    return tile[0:1, :] * 16.0 + tile[1:2, :]


def attend_kernel(heads, tokens, groups, n_buf, first, last, *refs):
    refs = list(refs)
    qs = [refs.pop(0) for _ in range(groups)]
    qids = [refs.pop(0) for _ in range(groups)]
    bufs = [refs.pop(0) for _ in range(n_buf)]
    carry = [] if first else [(refs.pop(0), refs.pop(0)) for _ in range(groups)]
    if last:
        outs = [refs.pop(0) for _ in range(groups)]
    else:
        outs = [(refs.pop(0), refs.pop(0)) for _ in range(groups)]
    bias = refs.pop(0)
    full = heads * tokens
    at = 2 * full
    scale = 1.0 / (math.sqrt(HD) * math.log(2.0))
    query_ids = jnp.concatenate([id_row(q, at) for q in qids], axis=1)
    for b in range(n_buf):
        column = jnp.broadcast_to(id_row(bufs[b], at), (tokens, tokens)).T
        column = jnp.concatenate([column] * groups, axis=1)
        bias[b * tokens : (b + 1) * tokens, :] = jnp.where(column == query_ids, 0.0, NEG)
    q_base = [0 if q.shape[0] == full else 2 * full + 16 for q in qs]
    for head in range(heads):
        rows = slice(head * tokens, (head + 1) * tokens)
        v_rows = slice(full + head * tokens, full + (head + 1) * tokens)
        keys = jnp.concatenate([b[rows, :] for b in bufs], axis=0)
        vals = jnp.concatenate([b[v_rows, :] for b in bufs], axis=1)
        query = jnp.concatenate(
            [q[base + head * tokens : base + (head + 1) * tokens, :] for q, base in zip(qs, q_base)], axis=0
        )
        s = lax.dot_general(keys, query, (((1,), (1,)), ((), ())), preferred_element_type=F32)
        s = s * scale + bias[...]
        m = jnp.max(s, axis=0, keepdims=True)
        if not first:
            old_m = jnp.concatenate([stat[head : head + 1, :] for _, stat in carry], axis=1)
            old_l = jnp.concatenate([stat[heads + head : heads + head + 1, :] for _, stat in carry], axis=1)
            old_acc = jnp.concatenate([acc[rows, :] for acc, _ in carry], axis=1)
            m = jnp.maximum(m, old_m)
            alpha = jnp.exp2(old_m - m)
        p = jnp.exp2(s - m)
        l = jnp.sum(p, axis=0, keepdims=True)
        acc = jnp.dot(vals, p.astype(BF16), preferred_element_type=F32)
        if not first:
            l = l + alpha * old_l
            acc = acc + alpha * old_acc
        if last:
            acc = acc * (1.0 / l)
        for g in range(groups):
            lanes = slice(g * tokens, (g + 1) * tokens)
            if last:
                outs[g][rows, :] = acc[:, lanes].T.astype(BF16)
            else:
                new_acc, new_stat = outs[g]
                new_acc[rows, :] = acc[:, lanes]
                new_stat[head : head + 1, :] = m[:, lanes]
                new_stat[heads + head : heads + head + 1, :] = l[:, lanes]


def attend(heads, qs, qids, bufs, carry, last):
    groups, n_buf, tokens = len(qs), len(bufs), HD
    rows = heads * tokens
    first = not carry
    flat_carry = [x for pair in carry for x in pair]
    if last:
        shapes = [jax.ShapeDtypeStruct((rows, HD), BF16) for _ in range(groups)]
    else:
        shapes = [jax.ShapeDtypeStruct((n, tokens), F32) for _ in range(groups) for n in (rows, 2 * heads)]
    vmem = pl.BlockSpec(memory_space=pltpu.VMEM)
    elements = groups * rows * n_buf * tokens
    out = pl.pallas_call(
        functools.partial(attend_kernel, heads, tokens, groups, n_buf, first, last),
        in_specs=[vmem] * (2 * groups + n_buf + len(flat_carry)),
        out_specs=[vmem] * len(shapes),
        out_shape=shapes,
        scratch_shapes=[pltpu.VMEM((n_buf * tokens, groups * tokens), F32)],
        cost_estimate=pl.CostEstimate(
            flops=elements * 512, bytes_accessed=n_buf * rows * 512 + groups * rows * 1024, transcendentals=elements
        ),
        compiler_params=pltpu.CompilerParams(vmem_limit_bytes=VMEM_LIMIT),
    )(*qs, *qids, *bufs, *flat_carry)
    if last:
        return out
    return [(out[2 * g], out[2 * g + 1]) for g in range(groups)]


def place_kernel(core_ref, o_mine, o_back, out_ref):
    tokens = out_ref.shape[0]
    half = out_ref.shape[1] // 2
    heads = half // HD
    core = core_ref[0]
    for side in range(2):
        @pl.when(core == side)
        def _():
            for head in range(heads):
                rows = slice(head * tokens, (head + 1) * tokens)
                a = side * half + head * HD
                b = (1 - side) * half + head * HD
                out_ref[:, a : a + HD] = o_mine[rows, :]
                out_ref[:, b : b + HD] = o_back[rows, :]


def place(core, o_mine, o_back, tokens, width):
    vmem = pl.BlockSpec(memory_space=pltpu.VMEM)
    return pl.pallas_call(
        place_kernel,
        in_specs=[pl.BlockSpec(memory_space=pltpu.SMEM), vmem, vmem],
        out_specs=vmem,
        out_shape=jax.ShapeDtypeStruct((tokens, width), BF16),
        compiler_params=pltpu.CompilerParams(vmem_limit_bytes=VMEM_LIMIT),
        name="place",
    )(core, o_mine, o_back)


def layer(queries, key_feats, value_feats, segment_ids):
    count = lax.axis_size(AXES)
    tokens, width = queries.shape
    core = lax.axis_index("head") % 2
    core_arr = core.reshape(1).astype(jnp.int32)

    chips = count // 2

    def swap(x):
        return lax.ppermute(x, AXES, [(d, d ^ 1) for d in range(count)])

    def pair_a(x, cross=0):
        return lax.ppermute(x, AXES, [(d, d ^ 2 ^ cross) for d in range(count)])

    def pair_b(x, cross=0):
        ups = [(2 * c + i, 2 * c + 2 + (i ^ cross)) for c in range(1, chips - 1, 2) for i in range(2)]
        return lax.ppermute(x, AXES, ups + [(v, u) for u, v in ups])

    kv, kvo, kvq, q = pack(core_arr, queries, key_feats, value_feats, segment_ids.reshape(1, tokens))
    b1 = pair_b(kv)
    a1 = pair_a(kv)
    b1x = pair_b(kvo, 1)
    a1x = pair_a(kvo, 1)
    kvq2 = swap(kvq)
    b2 = pair_b(a1)
    a2 = pair_a(b1)
    heads = width // 2 // HD
    qs, qids = [q, kvq2], [kv, kvq2]
    carry = attend(heads, qs, qids, [kv, kvq2, a1, b1], [], False)
    a1x, b1x, carry = lax.optimization_barrier((a1x, b1x, carry))
    b2x = pair_b(a1x)
    a2x = pair_a(b1x)
    carry = attend(heads, qs, qids, [a1x, b1x, a2, b2], carry, False)
    (o_other,) = attend(heads, [kvq2], [kvq2], [a2x, b2x], [carry[1]], True)
    back = swap(o_other)
    (o_mine,) = attend(heads, [q], [kv], [a2x, b2x], [carry[0]], True)
    return place(core_arr, o_mine, back, tokens, width)


def solution(mesh):
    return jax.shard_map(
        layer,
        mesh=mesh,
        in_specs=(
            P(("blk", "head"), None),
            P(("blk", "head"), None),
            P(("blk", "head"), None),
            P(("blk", "head")),
        ),
        out_specs=P(("blk", "head"), None),
        check_vma=False,
    )
```

```python
import functools
import math

import jax
import jax.numpy as jnp
from jax import lax
from jax.experimental import pallas as pl
from jax.experimental.pallas import tpu as pltpu
from jax.sharding import PartitionSpec as P


HD = 128
AXES = ("blk", "head")
NEG = -1e30
VMEM_LIMIT = 16 << 20
F32 = jnp.float32
BF16 = jnp.bfloat16


def load_halves(loads, sems):
    copies = []
    for n, (source, half_index, dest, at) in enumerate(loads):
        tokens, width = source.shape
        heads = width // 2 // HD
        for head in range(heads):
            first_col = pl.multiple_of(half_index * (width // 2) + head * HD, HD)
            rows = slice(at + head * tokens, at + (head + 1) * tokens)
            copy = pltpu.make_async_copy(source.at[:, pl.ds(first_col, HD)], dest.at[rows, :], sems.at[n, head])
            copy.start()
            copies.append(copy)
    return copies


def finish_pack(ids_ref, v_buf, out_refs, v_copies):
    tokens = ids_ref.shape[1]
    heads = v_buf.shape[0] // tokens
    full = heads * tokens
    ids = ids_ref[...] + 1
    row = lax.broadcasted_iota(jnp.int32, (16, tokens), 0)
    tile = jnp.where(row == 0, ids >> 4, jnp.where(row == 1, ids & 15, 0)).astype(F32).astype(BF16)
    for out_ref in out_refs:
        out_ref[2 * full : 2 * full + 16, :] = tile
    for head in range(heads):
        v_copies[head].wait()
        rows = head * tokens
        turned = v_buf[rows : rows + tokens, :].T
        for out_ref in out_refs:
            out_ref[full + rows : full + rows + tokens, :] = turned


def pack_mine_kernel(core_ref, k_hbm, v_hbm, ids_hbm, out_ref, v_buf, ids_buf, sems, id_sem):
    core = core_ref[0]
    heads = k_hbm.shape[1] // 2 // HD
    id_copy = pltpu.make_async_copy(ids_hbm, ids_buf, id_sem)
    id_copy.start()
    copies = load_halves([(v_hbm, core, v_buf, 0), (k_hbm, core, out_ref, 0)], sems)
    id_copy.wait()
    finish_pack(ids_buf, v_buf, [out_ref], copies[:heads])
    for copy in copies[heads:]:
        copy.wait()


def pack_other_kernel(core_ref, k_hbm, v_hbm, q_hbm, ids_hbm, kv_ref, kvq_ref, q_out, v_buf, ids_buf, sems, id_sem):
    core = core_ref[0]
    tokens = k_hbm.shape[0]
    heads = k_hbm.shape[1] // 2 // HD
    at = 2 * heads * tokens + 16
    id_copy = pltpu.make_async_copy(ids_hbm, ids_buf, id_sem)
    id_copy.start()
    loads = [
        (v_hbm, 1 - core, v_buf, 0),
        (k_hbm, 1 - core, kv_ref, 0),
        (k_hbm, 1 - core, kvq_ref, 0),
        (q_hbm, 1 - core, kvq_ref, at),
        (q_hbm, core, q_out, 0),
    ]
    copies = load_halves(loads, sems)
    id_copy.wait()
    finish_pack(ids_buf, v_buf, [kv_ref, kvq_ref], copies[:heads])
    for copy in copies[heads:]:
        copy.wait()


def pack(core, queries, keys, values, ids):
    tokens, width = queries.shape
    heads = width // 2 // HD
    rows = heads * tokens
    hbm = pl.BlockSpec(memory_space=pltpu.HBM)
    vmem = pl.BlockSpec(memory_space=pltpu.VMEM)

    def call(kernel, n_loads, sizes, limit, *args):
        return pl.pallas_call(
            kernel,
            in_specs=[pl.BlockSpec(memory_space=pltpu.SMEM)] + [hbm] * len(args),
            out_specs=[vmem for n in sizes],
            out_shape=[jax.ShapeDtypeStruct((n, HD), BF16) for n in sizes],
            scratch_shapes=[
                pltpu.VMEM((rows, HD), BF16),
                pltpu.VMEM((1, tokens), jnp.int32),
                pltpu.SemaphoreType.DMA((n_loads, heads)),
                pltpu.SemaphoreType.DMA(()),
            ],
            compiler_params=pltpu.CompilerParams(vmem_limit_bytes=limit),
        )(core, *args)

    keys, values, queries, ids = (pltpu.with_memory_space_constraint(x, pltpu.HBM) for x in (keys, values, queries, ids))
    (kv,) = call(pack_mine_kernel, 2, [2 * rows + 16], VMEM_LIMIT, keys, values, ids)
    keys, values, queries, kv = lax.optimization_barrier((keys, values, queries, kv))
    kvo, kvq, q = call(pack_other_kernel, 5, [2 * rows + 16, 3 * rows + 16, rows], VMEM_LIMIT, keys, values, queries, ids)
    return kv, kvo, kvq, q


def id_row(ref, at):
    tile = ref[at : at + 16, :].astype(F32)
    return tile[0:1, :] * 16.0 + tile[1:2, :]


def attend_kernel(heads, tokens, groups, n_buf, first, last, *refs):
    refs = list(refs)
    qs = [refs.pop(0) for _ in range(groups)]
    qids = [refs.pop(0) for _ in range(groups)]
    bufs = [refs.pop(0) for _ in range(n_buf)]
    carry = [] if first else [(refs.pop(0), refs.pop(0)) for _ in range(groups)]
    if last:
        outs = [refs.pop(0) for _ in range(groups)]
    else:
        outs = [(refs.pop(0), refs.pop(0)) for _ in range(groups)]
    bias = refs.pop(0)
    full = heads * tokens
    at = 2 * full
    scale = 1.0 / (math.sqrt(HD) * math.log(2.0))
    query_ids = jnp.concatenate([id_row(q, at) for q in qids], axis=1)
    for b in range(n_buf):
        column = jnp.broadcast_to(id_row(bufs[b], at), (tokens, tokens)).T
        column = jnp.concatenate([column] * groups, axis=1)
        bias[b * tokens : (b + 1) * tokens, :] = jnp.where(column == query_ids, 0.0, NEG)
    q_base = [0 if q.shape[0] == full else 2 * full + 16 for q in qs]
    for head in range(heads):
        rows = slice(head * tokens, (head + 1) * tokens)
        v_rows = slice(full + head * tokens, full + (head + 1) * tokens)
        keys = jnp.concatenate([b[rows, :] for b in bufs], axis=0)
        vals = jnp.concatenate([b[v_rows, :] for b in bufs], axis=1)
        query = jnp.concatenate(
            [q[base + head * tokens : base + (head + 1) * tokens, :] for q, base in zip(qs, q_base)], axis=0
        )
        s = lax.dot_general(keys, query, (((1,), (1,)), ((), ())), preferred_element_type=F32)
        s = s * scale + bias[...]
        m = jnp.max(s, axis=0, keepdims=True)
        if not first:
            old_m = jnp.concatenate([stat[head : head + 1, :] for _, stat in carry], axis=1)
            old_l = jnp.concatenate([stat[heads + head : heads + head + 1, :] for _, stat in carry], axis=1)
            old_acc = jnp.concatenate([acc[rows, :] for acc, _ in carry], axis=1)
            m = jnp.maximum(m, old_m)
            alpha = jnp.exp2(old_m - m)
        p = jnp.exp2(s - m)
        l = jnp.sum(p, axis=0, keepdims=True)
        acc = jnp.dot(vals, p.astype(BF16), preferred_element_type=F32)
        if not first:
            l = l + alpha * old_l
            acc = acc + alpha * old_acc
        if last:
            acc = acc * (1.0 / l)
        for g in range(groups):
            lanes = slice(g * tokens, (g + 1) * tokens)
            if last:
                outs[g][rows, :] = acc[:, lanes].T.astype(BF16)
            else:
                new_acc, new_stat = outs[g]
                new_acc[rows, :] = acc[:, lanes]
                new_stat[head : head + 1, :] = m[:, lanes]
                new_stat[heads + head : heads + head + 1, :] = l[:, lanes]


def attend(heads, qs, qids, bufs, carry, last):
    groups, n_buf, tokens = len(qs), len(bufs), HD
    rows = heads * tokens
    first = not carry
    flat_carry = [x for pair in carry for x in pair]
    if last:
        shapes = [jax.ShapeDtypeStruct((rows, HD), BF16) for _ in range(groups)]
    else:
        shapes = [jax.ShapeDtypeStruct((n, tokens), F32) for _ in range(groups) for n in (rows, 2 * heads)]
    vmem = pl.BlockSpec(memory_space=pltpu.VMEM)
    elements = groups * rows * n_buf * tokens
    out = pl.pallas_call(
        functools.partial(attend_kernel, heads, tokens, groups, n_buf, first, last),
        in_specs=[vmem] * (2 * groups + n_buf + len(flat_carry)),
        out_specs=[vmem] * len(shapes),
        out_shape=shapes,
        scratch_shapes=[pltpu.VMEM((n_buf * tokens, groups * tokens), F32)],
        cost_estimate=pl.CostEstimate(
            flops=elements * 512, bytes_accessed=n_buf * rows * 512 + groups * rows * 1024, transcendentals=elements
        ),
        compiler_params=pltpu.CompilerParams(vmem_limit_bytes=VMEM_LIMIT),
    )(*qs, *qids, *bufs, *flat_carry)
    if last:
        return out
    return [(out[2 * g], out[2 * g + 1]) for g in range(groups)]


def place_kernel(core_ref, o_mine, o_back, out_ref):
    tokens = out_ref.shape[0]
    half = out_ref.shape[1] // 2
    heads = half // HD
    core = core_ref[0]
    for side in range(2):
        @pl.when(core == side)
        def _():
            for head in range(heads):
                rows = slice(head * tokens, (head + 1) * tokens)
                a = side * half + head * HD
                b = (1 - side) * half + head * HD
                out_ref[:, a : a + HD] = o_mine[rows, :]
                out_ref[:, b : b + HD] = o_back[rows, :]


def place(core, o_mine, o_back, tokens, width):
    vmem = pl.BlockSpec(memory_space=pltpu.VMEM)
    return pl.pallas_call(
        place_kernel,
        in_specs=[pl.BlockSpec(memory_space=pltpu.SMEM), vmem, vmem],
        out_specs=vmem,
        out_shape=jax.ShapeDtypeStruct((tokens, width), BF16),
        compiler_params=pltpu.CompilerParams(vmem_limit_bytes=VMEM_LIMIT),
        name="place",
    )(core, o_mine, o_back)


def layer(queries, key_feats, value_feats, segment_ids):
    count = lax.axis_size(AXES)
    tokens, width = queries.shape
    core = lax.axis_index("head") % 2
    core_arr = core.reshape(1).astype(jnp.int32)

    chips = count // 2

    def swap(x):
        return lax.ppermute(x, AXES, [(d, d ^ 1) for d in range(count)])

    def pair_a(x, cross=0):
        return lax.ppermute(x, AXES, [(d, d ^ 2 ^ cross) for d in range(count)])

    def pair_b(x, cross=0):
        ups = [(2 * c + i, 2 * c + 2 + (i ^ cross)) for c in range(1, chips - 1, 2) for i in range(2)]
        return lax.ppermute(x, AXES, ups + [(v, u) for u, v in ups])

    kv, kvo, kvq, q = pack(core_arr, queries, key_feats, value_feats, segment_ids.reshape(1, tokens))
    b1 = pair_b(kv)
    a1 = pair_a(kv)
    b1x = pair_b(kvo, 1)
    a1x = pair_a(kvo, 1)
    kvq2 = swap(kvq)
    b2 = pair_b(a1)
    a2 = pair_a(b1)
    heads = width // 2 // HD
    qs, qids = [q, kvq2], [kv, kvq2]
    b2x = pair_b(a1x)
    a2x = pair_a(b1x)
    carry = attend(heads, qs, qids, [kv, kvq2, a1, b1], [], False)
    carry = attend(heads, qs, qids, [a1x, b1x, a2, b2], carry, False)
    (o_other,) = attend(heads, [kvq2], [kvq2], [a2x, b2x], [carry[1]], True)
    back = swap(o_other)
    (o_mine,) = attend(heads, [q], [kv], [a2x, b2x], [carry[0]], True)
    return place(core_arr, o_mine, back, tokens, width)


def solution(mesh):
    return jax.shard_map(
        layer,
        mesh=mesh,
        in_specs=(
            P(("blk", "head"), None),
            P(("blk", "head"), None),
            P(("blk", "head"), None),
            P(("blk", "head")),
        ),
        out_specs=P(("blk", "head"), None),
        check_vma=False,
    )
```

```python
import functools
import math

import jax
import jax.numpy as jnp
from jax import lax
from jax.experimental import pallas as pl
from jax.experimental.pallas import tpu as pltpu
from jax.sharding import PartitionSpec as P


HD = 128
AXES = ("blk", "head")
NEG = -1e30
VMEM_LIMIT = 16 << 20
F32 = jnp.float32
BF16 = jnp.bfloat16


def load_halves(loads, sems):
    copies = []
    for n, (source, half_index, dest, at) in enumerate(loads):
        tokens, width = source.shape
        heads = width // 2 // HD
        for head in range(heads):
            first_col = pl.multiple_of(half_index * (width // 2) + head * HD, HD)
            rows = slice(at + head * tokens, at + (head + 1) * tokens)
            copy = pltpu.make_async_copy(source.at[:, pl.ds(first_col, HD)], dest.at[rows, :], sems.at[n, head])
            copy.start()
            copies.append(copy)
    return copies


def finish_pack(ids_ref, v_buf, out_refs, v_copies):
    tokens = ids_ref.shape[1]
    heads = v_buf.shape[0] // tokens
    full = heads * tokens
    ids = ids_ref[...] + 1
    row = lax.broadcasted_iota(jnp.int32, (16, tokens), 0)
    tile = jnp.where(row == 0, ids >> 4, jnp.where(row == 1, ids & 15, 0)).astype(F32).astype(BF16)
    for out_ref in out_refs:
        out_ref[2 * full : 2 * full + 16, :] = tile
    for head in range(heads):
        v_copies[head].wait()
        rows = head * tokens
        turned = v_buf[rows : rows + tokens, :].T
        for out_ref in out_refs:
            out_ref[full + rows : full + rows + tokens, :] = turned


def pack_mine_kernel(core_ref, k_hbm, v_hbm, ids_hbm, out_ref, v_buf, ids_buf, sems, id_sem):
    core = core_ref[0]
    heads = k_hbm.shape[1] // 2 // HD
    id_copy = pltpu.make_async_copy(ids_hbm, ids_buf, id_sem)
    id_copy.start()
    copies = load_halves([(v_hbm, core, v_buf, 0), (k_hbm, core, out_ref, 0)], sems)
    id_copy.wait()
    finish_pack(ids_buf, v_buf, [out_ref], copies[:heads])
    for copy in copies[heads:]:
        copy.wait()


def pack_other_kernel(core_ref, k_hbm, v_hbm, q_hbm, ids_hbm, kv_ref, kvq_ref, q_out, v_buf, ids_buf, sems, id_sem):
    core = core_ref[0]
    tokens = k_hbm.shape[0]
    heads = k_hbm.shape[1] // 2 // HD
    at = 2 * heads * tokens + 16
    id_copy = pltpu.make_async_copy(ids_hbm, ids_buf, id_sem)
    id_copy.start()
    loads = [
        (v_hbm, 1 - core, v_buf, 0),
        (k_hbm, 1 - core, kv_ref, 0),
        (k_hbm, 1 - core, kvq_ref, 0),
        (q_hbm, 1 - core, kvq_ref, at),
        (q_hbm, core, q_out, 0),
    ]
    copies = load_halves(loads, sems)
    id_copy.wait()
    finish_pack(ids_buf, v_buf, [kv_ref, kvq_ref], copies[:heads])
    for copy in copies[heads:]:
        copy.wait()


def pack(core, queries, keys, values, ids):
    tokens, width = queries.shape
    heads = width // 2 // HD
    rows = heads * tokens
    hbm = pl.BlockSpec(memory_space=pltpu.HBM)
    vmem = pl.BlockSpec(memory_space=pltpu.VMEM)

    def call(kernel, n_loads, sizes, limit, *args):
        return pl.pallas_call(
            kernel,
            in_specs=[pl.BlockSpec(memory_space=pltpu.SMEM)] + [hbm] * len(args),
            out_specs=[vmem for n in sizes],
            out_shape=[jax.ShapeDtypeStruct((n, HD), BF16) for n in sizes],
            scratch_shapes=[
                pltpu.VMEM((rows, HD), BF16),
                pltpu.VMEM((1, tokens), jnp.int32),
                pltpu.SemaphoreType.DMA((n_loads, heads)),
                pltpu.SemaphoreType.DMA(()),
            ],
            compiler_params=pltpu.CompilerParams(vmem_limit_bytes=limit),
        )(core, *args)

    keys, values, queries, ids = (pltpu.with_memory_space_constraint(x, pltpu.HBM) for x in (keys, values, queries, ids))
    (kv,) = call(pack_mine_kernel, 2, [2 * rows + 16], VMEM_LIMIT, keys, values, ids)
    keys, values, queries, kv = lax.optimization_barrier((keys, values, queries, kv))
    kvo, kvq, q = call(pack_other_kernel, 5, [2 * rows + 16, 3 * rows + 16, rows], VMEM_LIMIT, keys, values, queries, ids)
    return kv, kvo, kvq, q


def id_row(ref, at):
    tile = ref[at : at + 16, :].astype(F32)
    return tile[0:1, :] * 16.0 + tile[1:2, :]


def attend_kernel(heads, tokens, groups, n_buf, first, last, direct, *refs):
    refs = list(refs)
    core = refs.pop(0)[0] if direct else None
    qs = [refs.pop(0) for _ in range(groups)]
    qids = [refs.pop(0) for _ in range(groups)]
    bufs = [refs.pop(0) for _ in range(n_buf)]
    carry = [] if first else [(refs.pop(0), refs.pop(0)) for _ in range(groups)]
    if last:
        outs = [refs.pop(0) for _ in range(groups)]
    else:
        outs = [(refs.pop(0), refs.pop(0)) for _ in range(groups)]
    bias = refs.pop(0)
    if direct:
        o_buf, sems = refs
        copies = []
    full = heads * tokens
    at = 2 * full
    scale = 1.0 / (math.sqrt(HD) * math.log(2.0))
    query_ids = jnp.concatenate([id_row(q, at) for q in qids], axis=1)
    for b in range(n_buf):
        column = jnp.broadcast_to(id_row(bufs[b], at), (tokens, tokens)).T
        column = jnp.concatenate([column] * groups, axis=1)
        bias[b * tokens : (b + 1) * tokens, :] = jnp.where(column == query_ids, 0.0, NEG)
    q_base = [0 if q.shape[0] == full else 2 * full + 16 for q in qs]
    for head in range(heads):
        rows = slice(head * tokens, (head + 1) * tokens)
        v_rows = slice(full + head * tokens, full + (head + 1) * tokens)
        keys = jnp.concatenate([b[rows, :] for b in bufs], axis=0)
        vals = jnp.concatenate([b[v_rows, :] for b in bufs], axis=1)
        query = jnp.concatenate(
            [q[base + head * tokens : base + (head + 1) * tokens, :] for q, base in zip(qs, q_base)], axis=0
        )
        s = lax.dot_general(keys, query, (((1,), (1,)), ((), ())), preferred_element_type=F32)
        s = s * scale + bias[...]
        m = jnp.max(s, axis=0, keepdims=True)
        if not first:
            old_m = jnp.concatenate([stat[head : head + 1, :] for _, stat in carry], axis=1)
            old_l = jnp.concatenate([stat[heads + head : heads + head + 1, :] for _, stat in carry], axis=1)
            old_acc = jnp.concatenate([acc[rows, :] for acc, _ in carry], axis=1)
            m = jnp.maximum(m, old_m)
            alpha = jnp.exp2(old_m - m)
        p = jnp.exp2(s - m)
        l = jnp.sum(p, axis=0, keepdims=True)
        acc = jnp.dot(vals, p.astype(BF16), preferred_element_type=F32)
        if not first:
            l = l + alpha * old_l
            acc = acc + alpha * old_acc
        if last:
            acc = acc * (1.0 / l)
        for g in range(groups):
            lanes = slice(g * tokens, (g + 1) * tokens)
            if direct:
                o_buf[rows, :] = acc[:, lanes].T.astype(BF16)
                copies.append(put_head(o_buf, rows, outs[g], core, head, sems))
            elif last:
                outs[g][rows, :] = acc[:, lanes].T.astype(BF16)
            else:
                new_acc, new_stat = outs[g]
                new_acc[rows, :] = acc[:, lanes]
                new_stat[head : head + 1, :] = m[:, lanes]
                new_stat[heads + head : heads + head + 1, :] = l[:, lanes]
    if direct:
        for copy in copies:
            copy.wait()


def put_head(source, rows, out_ref, side, head, sems):
    first_col = pl.multiple_of(side * (out_ref.shape[1] // 2) + head * HD, HD)
    copy = pltpu.make_async_copy(source.at[rows, :], out_ref.at[:, pl.ds(first_col, HD)], sems.at[head])
    copy.start()
    return copy


def attend(heads, qs, qids, bufs, carry, last, direct=None):
    groups, n_buf, tokens = len(qs), len(bufs), HD
    rows = heads * tokens
    first = not carry
    flat_carry = [x for pair in carry for x in pair]
    if last:
        shapes = [jax.ShapeDtypeStruct((rows, HD), BF16) for _ in range(groups)]
    else:
        shapes = [jax.ShapeDtypeStruct((n, tokens), F32) for _ in range(groups) for n in (rows, 2 * heads)]
    vmem = pl.BlockSpec(memory_space=pltpu.VMEM)
    first_specs, out_specs, more_scratch, first_args = [], [vmem] * len(shapes), [], ()
    if direct is not None:
        shapes = [jax.ShapeDtypeStruct((tokens, 2 * rows), BF16)]
        first_specs, out_specs = [pl.BlockSpec(memory_space=pltpu.SMEM)], [pl.BlockSpec(memory_space=pltpu.HBM)]
        more_scratch = [pltpu.VMEM((rows, HD), BF16), pltpu.SemaphoreType.DMA((heads,))]
        first_args = (direct,)
    elements = groups * rows * n_buf * tokens
    out = pl.pallas_call(
        functools.partial(attend_kernel, heads, tokens, groups, n_buf, first, last, direct is not None),
        in_specs=first_specs + [vmem] * (2 * groups + n_buf + len(flat_carry)),
        out_specs=out_specs,
        out_shape=shapes,
        scratch_shapes=[pltpu.VMEM((n_buf * tokens, groups * tokens), F32)] + more_scratch,
        cost_estimate=pl.CostEstimate(
            flops=elements * 512, bytes_accessed=n_buf * rows * 512 + groups * rows * 1024, transcendentals=elements
        ),
        compiler_params=pltpu.CompilerParams(vmem_limit_bytes=VMEM_LIMIT),
    )(*first_args, *qs, *qids, *bufs, *flat_carry)
    if last:
        return out
    return [(out[2 * g], out[2 * g + 1]) for g in range(groups)]


def place_kernel(core_ref, o_back, half_done, out_ref, sems):
    tokens = out_ref.shape[0]
    heads = o_back.shape[0] // tokens
    other = 1 - core_ref[0]
    copies = [
        put_head(o_back, slice(head * tokens, (head + 1) * tokens), out_ref, other, head, sems) for head in range(heads)
    ]
    for copy in copies:
        copy.wait()


def place(core, o_back, half_done):
    hbm = pl.BlockSpec(memory_space=pltpu.HBM)
    return pl.pallas_call(
        place_kernel,
        in_specs=[pl.BlockSpec(memory_space=pltpu.SMEM), pl.BlockSpec(memory_space=pltpu.VMEM), hbm],
        out_specs=hbm,
        out_shape=jax.ShapeDtypeStruct(half_done.shape, BF16),
        scratch_shapes=[pltpu.SemaphoreType.DMA((o_back.shape[0] // half_done.shape[0],))],
        input_output_aliases={2: 0},
        compiler_params=pltpu.CompilerParams(vmem_limit_bytes=VMEM_LIMIT),
        name="place",
    )(core, o_back, half_done)


def layer(queries, key_feats, value_feats, segment_ids):
    count = lax.axis_size(AXES)
    tokens, width = queries.shape
    core = lax.axis_index("head") % 2
    core_arr = core.reshape(1).astype(jnp.int32)

    chips = count // 2

    def swap(x):
        return lax.ppermute(x, AXES, [(d, d ^ 1) for d in range(count)])

    def pair_a(x, cross=0):
        return lax.ppermute(x, AXES, [(d, d ^ 2 ^ cross) for d in range(count)])

    def pair_b(x, cross=0):
        ups = [(2 * c + i, 2 * c + 2 + (i ^ cross)) for c in range(1, chips - 1, 2) for i in range(2)]
        return lax.ppermute(x, AXES, ups + [(v, u) for u, v in ups])

    kv, kvo, kvq, q = pack(core_arr, queries, key_feats, value_feats, segment_ids.reshape(1, tokens))
    b1 = pair_b(kv)
    a1 = pair_a(kv)
    b1x = pair_b(kvo, 1)
    a1x = pair_a(kvo, 1)
    kvq2 = swap(kvq)
    b2 = pair_b(a1)
    a2 = pair_a(b1)
    heads = width // 2 // HD
    qs, qids = [q, kvq2], [kv, kvq2]
    b2x = pair_b(a1x)
    a2x = pair_a(b1x)
    carry = attend(heads, qs, qids, [kv, kvq2, a1, b1], [], False)
    carry = attend(heads, qs, qids, [a1x, b1x, a2, b2], carry, False)
    carry = attend(heads, qs, qids, [a2x], carry, False)
    (o_other,) = attend(heads, [kvq2], [kvq2], [b2x], [carry[1]], True)
    back = swap(o_other)
    (half_done,) = attend(heads, [q], [kv], [b2x], [carry[0]], True, core_arr)
    return place(core_arr, back, half_done)


def solution(mesh):
    return jax.shard_map(
        layer,
        mesh=mesh,
        in_specs=(
            P(("blk", "head"), None),
            P(("blk", "head"), None),
            P(("blk", "head"), None),
            P(("blk", "head")),
        ),
        out_specs=P(("blk", "head"), None),
        check_vma=False,
    )
```
